32 devices in a mesh: gx: 8 (over z, y), gy: 4 (over x, core).
Axes of the slice: x: 2, y: 2, z: 4, core: 2. Of those that a mesh axis runs over, the one named last changes fastest.
Arguments:
- right_side: float32 [7, 7, 7, 16, 16, 128], P(None, None, None, 'gx', 'gy'), may hold values from -6 to 6
- coefficient: float32 [16, 16, 128], P('gx', 'gy'), may hold values from 0.2 to 5
- degrees: int32 [3, 16, 16, 128], P(None, 'gx', 'gy'), may hold values from 2 to 6
Outputs:
- smoothed: float32 [7, 7, 7, 16, 16, 128], P(None, None, None, 'gx', 'gy')
- coarse_residual: float32 [64, 16, 2048], P(None, 'gx', 'gy')
The draws below stay inside these ranges and needn't reach their ends.
All inputs are finite; a program needn't handle non-finite values.
Results may differ from the reference program's by a relative error of at most 0.0003.
Values sent between devices are 32-bit elements; how exact they have to be, the bound alone decides.
A program may use at most 64 MiB of HBM per device.

```python
import math
import jax
import jax.numpy as jnp
from jax import lax

MODES = 7
CMODES = 4
SMOOTH = 3
NX = 16
NY = 16
NZ = 128


def place_ends(values, stream_key, least, top_value):
    longest = values.shape.index(max(values.shape))
    spots = []
    for shift in (0, 1):
        where = [jax.random.randint(jax.random.fold_in(stream_key, axis), (), 0, length) for axis, length in enumerate(values.shape)]
        where[longest] = (where[longest] + shift) % values.shape[longest]
        spots.append(tuple(where))
    return values.at[spots[0]].set(least).at[spots[1]].set(top_value)


def block_levels(rng, extent, split, least, top_value):
    loudness = 1.0
    for dim, parts in split:
        draws = jax.random.uniform(jax.random.fold_in(jax.random.fold_in(rng, 6), dim), (parts,), jnp.float32, least / len(split), top_value / len(split))
        loudness = loudness * jnp.repeat(jnp.exp(draws), extent[dim] // parts).reshape((-1,) + (1,) * (len(extent) - 1 - dim))
    return loudness


def noise(stream_key, dims, deviation, reach, split=(), kind=jnp.bfloat16):
    loudness = block_levels(stream_key, dims, split, -0.22, 0.18) if split else 1.0
    entries = jax.random.normal(stream_key, dims, jnp.float32) * deviation * loudness
    return jnp.minimum(jnp.maximum(entries, -reach), reach).astype(kind)


def setup_inputs(seed: int = 0) -> dict:
    seeds = jax.random.split(jax.random.key(seed), 4)
    return {
        "right_side": noise(seeds[0], (MODES, MODES, MODES, NX, NY, NZ), 1.0, 6.0, ((3, 8), (4, 4)), jnp.float32),
        "coefficient": jnp.clip(jnp.exp(math.log(5.0) - 3.218876 * jax.random.uniform(seeds[1], (NX, NY, NZ), jnp.float32) ** block_levels(seeds[1], (NX, NY, NZ), ((0, 8), (1, 4)), -0.2, 0.2)), 0.2, 5.0),
        "degrees": place_ends(jax.random.randint(seeds[2], (3, NX, NY, NZ), 2, 7), jax.random.fold_in(seeds[2], 1), 2, 6).astype(jnp.int32),
    }


lam_high = 6.0
lam_low = 0.5
exact_precision = lax.Precision.HIGHEST
TRACE_FORMS = ("ka,abgxyz->kbgxyz", "kb,abgxyz->kagxyz", "kg,abgxyz->kabxyz")
SPREAD_FORMS = ("ka,kbgxyz->abgxyz", "kb,kagxyz->abgxyz", "kg,kabxyz->abgxyz")
VOLUME_FORMS = ("ai,ibgxyz->abgxyz", "bi,aigxyz->abgxyz", "gi,abixyz->abgxyz")


def tables(mode_count):
    mode_index = jnp.arange(mode_count).astype(jnp.float32)
    parity = 1.0 - 2.0 * jnp.mod(mode_index, 2.0)
    slopes = mode_index * (mode_index + 1.0) / 2.0
    vectors = jnp.stack([jnp.ones_like(mode_index), slopes, parity, -parity * slopes])
    signs = jnp.array([1.0, -1.0, -1.0, -1.0], dtype=jnp.float32)
    signed = vectors * signs[:, None]
    masses = 2.0 / (2.0 * mode_index + 1.0)
    lesser = jnp.minimum(mode_index[:, None], mode_index[None, :])
    parity_even = jnp.mod(mode_index[:, None] + mode_index[None, :], 2.0) == 0.0
    stiffness = jnp.where(parity_even, lesser * (lesser + 1.0), 0.0).astype(jnp.float32)
    return vectors, signed, masses, stiffness, mode_index


def along(vector, direction):
    layout = [1, 1, 1, 1, 1, 1]
    layout[direction] = vector.shape[0]
    return vector.reshape(layout)


def edge_pad(rank, direction):
    widths = [(0, 0)] * rank
    widths[direction] = (1, 1)
    return widths


def degree_mask(degrees, mode_count):
    levels = jnp.arange(mode_count, dtype=jnp.int32)
    inside = (along(levels, 0) <= degrees[0]) & (along(levels, 1) <= degrees[1]) & (along(levels, 2) <= degrees[2])
    return jnp.where(inside, 1.0, 0.0).astype(jnp.float32)


def face_weight(offset, cell_count, length_total, direction):
    position = offset + jnp.arange(cell_count + 1, dtype=jnp.int32)
    inside = (position >= 1) & (position <= length_total - 1)
    weight = jnp.where(inside, 0.5, 1.0).astype(jnp.float32)
    layout = [1, 1, 1]
    layout[direction] = cell_count + 1
    return weight.reshape(layout)


def face_geometry(coef_pad, degree_pad, direction):
    length = coef_pad.shape[direction]
    left_coef = lax.slice_in_dim(coef_pad, 0, length - 1, axis=direction)
    right_coef = lax.slice_in_dim(coef_pad, 1, length, axis=direction)
    larger = jnp.maximum(lax.slice_in_dim(degree_pad, 0, length - 1, axis=direction),
                         lax.slice_in_dim(degree_pad, 1, length, axis=direction))
    penalty = jnp.maximum(left_coef, right_coef) * (larger + 1.0) * (larger + 2.0)
    return left_coef, right_coef, penalty


def scale_traces(traces, coef_pad):
    return jnp.stack([traces[0], traces[1] * coef_pad, traces[2], traces[3] * coef_pad])


def face_terms(traces, geometry, weight, direction, signed, tangent_mass):
    left_coef, right_coef, penalty = geometry
    spatial = 3 + direction
    length = traces.shape[3 + direction]

    def left_part(values):
        return lax.slice_in_dim(values, 0, length - 1, axis=spatial - 1)

    def right_part(values):
        return lax.slice_in_dim(values, 1, length, axis=spatial - 1)

    def upper_face(values):
        return lax.slice_in_dim(values, 1, length - 1, axis=spatial - 1)

    def lower_face(values):
        return lax.slice_in_dim(values, 0, length - 2, axis=spatial - 1)

    jump_term = left_part(traces[0]) - right_part(traces[2])
    flux_term = weight * (left_part(traces[1]) + right_part(traces[3]))
    across = penalty * jump_term - flux_term
    left_sym = weight * left_coef * jump_term
    right_sym = weight * right_coef * jump_term
    stacked = jnp.stack([upper_face(across), upper_face(left_sym), lower_face(across), lower_face(right_sym)]) * tangent_mass
    return jnp.einsum(SPREAD_FORMS[direction], signed, stacked, precision=exact_precision)


def volume(values, coefficient, masses, stiffness):
    mass_a, mass_b, mass_g = along(masses, 0), along(masses, 1), along(masses, 2)
    result = jnp.einsum(VOLUME_FORMS[0], stiffness, values, precision=exact_precision) * mass_b * mass_g
    result = result + jnp.einsum(VOLUME_FORMS[1], stiffness, values, precision=exact_precision) * mass_a * mass_g
    result = result + jnp.einsum(VOLUME_FORMS[2], stiffness, values, precision=exact_precision) * mass_a * mass_b
    return coefficient * result


def jacobi_inverse(coefficient, geometry, weights, masses, stiffness, mode_index, mask):
    mass_axes = (along(masses, 0), along(masses, 1), along(masses, 2))
    stiff_diag = jnp.diagonal(stiffness)
    result = coefficient * (along(stiff_diag, 0) * mass_axes[1] * mass_axes[2]
                            + mass_axes[0] * along(stiff_diag, 1) * mass_axes[2]
                            + mass_axes[0] * mass_axes[1] * along(stiff_diag, 2))
    for direction in range(3):
        others = [mass_axes[other] for other in range(3) if other != direction]
        penalty = geometry[direction][2]
        weight = weights[direction]
        length = penalty.shape[direction]
        penalty_sum = lax.slice_in_dim(penalty, 1, length, axis=direction) + lax.slice_in_dim(penalty, 0, length - 1, axis=direction)
        weight_sum = lax.slice_in_dim(weight, 1, length, axis=direction) + lax.slice_in_dim(weight, 0, length - 1, axis=direction)
        curvature = along(mode_index * (mode_index + 1.0), direction)
        result = result + others[0] * others[1] * (penalty_sum - weight_sum * coefficient * curvature)
    return mask / result


def restrict(residual, degrees, coarse_modes):
    levels = jnp.arange(coarse_modes, dtype=jnp.int32)
    halves = degrees // 2
    keep = (along(levels, 0) <= halves[0]) & (along(levels, 1) <= halves[1]) & (along(levels, 2) <= halves[2])
    kept = jnp.where(keep, residual[:coarse_modes, :coarse_modes, :coarse_modes], 0.0)
    return kept.reshape((coarse_modes * coarse_modes * coarse_modes,) + residual.shape[3:])


def reference(right_side, coefficient, degrees):
    vectors, signed, masses, stiffness, mode_index = tables(MODES)
    tangent_mass = masses[None, :, None, None, None, None] * masses[None, None, :, None, None, None]
    mask = degree_mask(degrees, MODES)
    source = right_side * mask
    degree_float = degrees.astype(jnp.float32)
    totals = (NX, NY, NZ)
    weights = [face_weight(0, totals[direction], totals[direction], direction) for direction in range(3)]
    coef_pads = [jnp.pad(coefficient, edge_pad(3, direction)) for direction in range(3)]
    geometry = [face_geometry(coef_pads[direction], jnp.pad(degree_float[direction], edge_pad(3, direction)), direction) for direction in range(3)]
    inverse = jacobi_inverse(coefficient, geometry, weights, masses, stiffness, mode_index, mask)

    def operator(values):
        result = volume(values, coefficient, masses, stiffness)
        for direction in range(3):
            padded = jnp.pad(values, edge_pad(6, 3 + direction))
            traces = jnp.einsum(TRACE_FORMS[direction], vectors, padded, precision=exact_precision)
            traces = scale_traces(traces, coef_pads[direction])
            result = result + face_terms(traces, geometry[direction], weights[direction], direction, signed, tangent_mass)
        return mask * result

    centre = (lam_high + lam_low) / 2.0
    radius = (lam_high - lam_low) / 2.0
    interval_ratio = centre / radius
    rho_now = 1.0 / interval_ratio
    step_term = inverse * source / centre
    solution = step_term
    for sweep_index in range(SMOOTH - 1):
        rho_next = 1.0 / (2.0 * interval_ratio - rho_now)
        residual = source - operator(solution)
        step_term = rho_next * rho_now * step_term + (2.0 * rho_next / radius) * inverse * residual
        solution = solution + step_term
        rho_now = rho_next
    residual = source - operator(solution)
    coarse = restrict(residual, degrees, CMODES)
    coarse = jnp.transpose(coarse, (0, 1, 3, 2)).reshape(CMODES * CMODES * CMODES, NX, NZ * NY)
    return solution, coarse
```

```python
import functools

import jax
import jax.numpy as jnp
from jax import lax
from jax.experimental import pallas as pl
from jax.experimental.pallas import tpu as pltpu
from jax.sharding import PartitionSpec as P

CMODES = 4
LAM_HIGH = 6.0
LAM_LOW = 0.5
MODES = 7
MESH = pl.DeviceIdType.MESH
F32 = jnp.float32
HALF = [(2.0 * n + 1.0) / 2.0 for n in range(MODES)]
SLOPE = [n * (n + 1.0) / 2.0 for n in range(MODES)]


def chebyshev():
    centre = (LAM_HIGH + LAM_LOW) / 2.0
    radius = (LAM_HIGH - LAM_LOW) / 2.0
    ratio = centre / radius
    rho = 1.0 / ratio
    pairs = []
    for _ in range(2):
        following = 1.0 / (2.0 * ratio - rho)
        pairs.append((following * rho, 2.0 * following / radius))
        rho = following
    return 1.0 / centre, pairs


def rows(shape):
    return lax.broadcasted_iota(jnp.int32, shape, len(shape) - 2)


def lanes(shape):
    return lax.broadcasted_iota(jnp.int32, shape, len(shape) - 1)


def turn(v, shift):
    return pltpu.roll(v, shift, v.ndim - 2)


def pack_x_up(p, q):
    return jnp.where(rows(p.shape) < 4, turn(p, 4), q)


def pack_x_down(p, q):
    return jnp.where(rows(p.shape) < 4, p, turn(q, 4))


def prev_x(p, q, g):
    low = rows(p.shape) < 4
    return jnp.where(low, g, turn(p, 4)), turn(jnp.where(low, q, g), 4)


def next_x(p, q, g):
    low = rows(p.shape) < 4
    return turn(jnp.where(low, g, p), 4), jnp.where(low, turn(q, 4), g)


def pack_y_up(p, q):
    return jnp.where((rows(p.shape) & 3) == 0, turn(p, 5), turn(q, 6))


def pack_y_down(p, q):
    return jnp.where((rows(p.shape) & 3) == 3, turn(p, 3), turn(q, 2))


def prev_y(p, q, g):
    edge = (rows(p.shape) & 3) == 0
    return jnp.where(edge, g, turn(p, 1)), jnp.where(edge, turn(g, 7), turn(q, 1))


def next_y(p, q, g):
    edge = (rows(p.shape) & 3) == 3
    return jnp.where(edge, g, turn(p, 7)), jnp.where(edge, turn(g, 1), turn(q, 7))


def prev_z(p):
    return jnp.where(lanes(p.shape) == 0, 0.0, pltpu.roll(p, 1, p.ndim - 1))


def next_z(p):
    end = p.shape[-1] - 1
    return jnp.where(lanes(p.shape) == end, 0.0, pltpu.roll(p, end, p.ndim - 1))


def line(u, half_coef):
    t4 = u[4] + u[6]
    t2 = u[2] + t4
    even = u[0] + t2
    t3 = u[3] + u[5]
    odd = u[1] + t3
    s2 = 6.0 * t2
    s4 = s2 + 14.0 * t4
    s6 = s4 + 22.0 * u[6]
    s1 = 2.0 * odd
    s3 = s1 + 10.0 * t3
    s5 = s3 + 18.0 * u[5]
    tp = even + odd
    tm = even - odd
    fp = half_coef * (s6 + s5)
    fm = half_coef * (s5 - s6)
    return (tp, tm, fp, fm), (None, s1, s2, s3, s4, s5, s6)


def spread(traces, before, after, geom, coef, sums, count):
    tp, tm, fp, fm = traces
    tau_a, tau_b, w_a, w_b, k_a, k_b = geom
    jump_a = tp - after[0]
    g_a = tau_a * jump_a - w_a * (fp + after[1])
    jump_b = before[0] - tm
    g_b = tau_b * jump_b - w_b * (before[1] + fm)
    kl = k_a * jump_a
    kr = k_b * jump_b
    p = (g_a - g_b, g_a + g_b)
    q = (kl - kr, kl + kr)
    out = [HALF[0] * p[0]]
    for n in range(1, count):
        out.append(HALF[n] * (coef * sums[n] + (p[n % 2] - SLOPE[n] * q[n % 2])))
    return out


def kernel(nx, ny, rhs, coef, deg, u, coarse, s, inv, step, acc, geo, dia, zm,
           ps, pg, xs, xg, ys, yg, xs3, xg3, ys3, yg3,
           p_send, p_recv, x_send, x_recv, y_send, y_recv):
    gx, gy = lax.axis_index("gx"), lax.axis_index("gy")
    exists = (gx < nx - 1, gx > 0, gy < ny - 1, gy > 0)
    target = ({"gx": gx + 1}, {"gx": gx - 1}, {"gy": gy + 1}, {"gy": gy - 1})
    source = (exists[1], exists[0], exists[3], exists[2])

    barrier = pltpu.get_barrier_semaphore()
    for d in range(4):
        @pl.when(exists[d])
        def _(d=d):
            pl.semaphore_signal(barrier, inc=1, device_id=target[d], device_id_type=MESH)

    def copy(src, dst, send, recv, d):
        return pltpu.make_async_remote_copy(src_ref=src, dst_ref=dst, send_sem=send, recv_sem=recv,
                                            device_id=target[d], device_id_type=MESH)

    def param_copy(d):
        return copy(ps.at[d], pg.at[d], p_send.at[d], p_recv.at[d], d)

    def x_copy(k, d, b):
        if k < 2:
            return copy(xs.at[k, d, b], xg.at[k, d, b], x_send.at[k, d, b], x_recv.at[k, d, b], d)
        return copy(xs3.at[d, b], xg3.at[d, b], x_send.at[k, d, b], x_recv.at[k, d, b], d)

    def y_copy(k, d, a):
        if k < 2:
            return copy(ys.at[k, d, a], yg.at[k, d, a], y_send.at[k, d, a], y_recv.at[k, d, a], 2 + d)
        return copy(ys3.at[d, a], yg3.at[d, a], y_send.at[k, d, a], y_recv.at[k, d, a], 2 + d)

    c = coef[...]
    half_coef = 0.5 * c
    df = [deg[d].astype(F32) for d in range(3)]
    ps[0] = pack_x_up(c, df[0])
    ps[1] = pack_x_down(c, df[0])
    ps[2] = pack_y_up(c, df[1])
    ps[3] = pack_y_down(c, df[1])
    pl.semaphore_wait(barrier, sum(e.astype(jnp.int32) for e in exists))
    for d in range(4):
        @pl.when(exists[d])
        def _(d=d):
            param_copy(d).start()

    for d in range(4):
        @pl.when(jnp.logical_not(source[d]))
        def _(d=d):
            pg[d] = jnp.zeros((8, 128), F32)
            ghosts = (xg, yg)[d // 2]
            ghosts3 = (xg3, yg3)[d // 2]

            def clear(i, _):
                for k in range(2):
                    ghosts[k, d % 2, i] = jnp.zeros((MODES, 8, 128), F32)
                return 0
            lax.fori_loop(0, MODES, clear, 0)

            def clear3(i, _):
                ghosts3[d % 2, i] = jnp.zeros((CMODES, 8, 128), F32)
                return 0
            lax.fori_loop(0, CMODES, clear3, 0)

    shape = (MODES, 8, 128)
    levels = lax.broadcasted_iota(jnp.int32, shape, 0)
    zm[...] = jnp.where(levels <= deg[2][None], 1.0, 0.0)

    def prepare(direction, before, after, first, last):
        degree = df[direction]
        wide_a = jnp.maximum(degree, after[1])
        wide_b = jnp.maximum(degree, before[1])
        tau_a = jnp.maximum(c, after[0]) * (wide_a + 1.0) * (wide_a + 2.0)
        tau_b = jnp.maximum(c, before[0]) * (wide_b + 1.0) * (wide_b + 2.0)
        w_a = jnp.where(last, 1.0, 0.5)
        w_b = jnp.where(first, 1.0, 0.5)
        for i, value in enumerate((tau_a, tau_b, w_a, w_b, w_a * c, w_b * c)):
            geo[direction, i] = value
        rest = (1.0 - (w_a + w_b)) * c
        for n in range(MODES):
            dia[direction, n] = HALF[n] * (tau_a + tau_b + (2.0 * SLOPE[n]) * rest)

    row, lane = rows((8, 128)), lanes((8, 128))
    prepare(2, (prev_z(c), prev_z(df[2])), (next_z(c), next_z(df[2])), lane == 0, lane == 127)
    for d in range(4):
        @pl.when(source[d])
        def _(d=d):
            param_copy(d).wait_recv()
    px, py = gx * 2 + (row >> 2), gy * 4 + (row & 3)
    prepare(0, prev_x(c, df[0], pg[0]), next_x(c, df[0], pg[1]), px == 0, px == 2 * nx - 1)
    prepare(1, prev_y(c, df[1], pg[2]), next_y(c, df[1], pg[3]), py == 0, py == 4 * ny - 1)

    first_scale, pairs = chebyshev()
    odds = 2.0 * levels.astype(F32) + 1.0

    def setup(a, _):
        for b in range(MODES):
            inside = jnp.where(deg[0] >= a, jnp.where(deg[1] >= b, 1.0, 0.0), 0.0)
            i = (inside[None] * zm[...]) / ((dia[0, a] + dia[1, b])[None] + dia[2])
            r = rhs[a, b] * (odds * ((2.0 * a.astype(F32) + 1.0) * ((2.0 * b + 1.0) / 8.0)))
            x = i * r * first_scale
            s[a, b] = r
            inv[a, b] = i
            step[a, b] = x
            u[a, b] = x
        return 0
    lax.fori_loop(0, MODES, setup, 0)

    def geom(direction):
        return tuple(geo[direction, i][None] for i in range(6))

    def start(make, k, at, base):
        for d in range(2):
            @pl.when(exists[base + d])
            def _(d=d):
                make(k, d, at).start()

    def arrive(make, k, at, base):
        for d in range(2):
            @pl.when(source[base + d])
            def _(d=d):
                make(k, d, at).wait_recv()

    def send_x(k, b, values):
        (tp, tm, fp, fm), _ = line(values, half_coef[None])
        up, down = pack_x_up(tp, fp), pack_x_down(tm, fm)
        if k < 2:
            xs[k, 0, b] = up
            xs[k, 1, b] = down
        else:
            xs3[0, b] = up
            xs3[1, b] = down
        start(x_copy, k, b, 0)

    def first_x(b, _):
        send_x(0, b, [u[n, b] for n in range(MODES)])
        return 0
    lax.fori_loop(0, MODES, first_x, 0)

    for k in range(3):
        count = MODES if k < 2 else CMODES

        def traces_y(a, _):
            (tp, tm, fp, fm), _ = line([u[a, n, 0:count] for n in range(MODES)], half_coef[None])
            up, down = pack_y_up(tp, fp), pack_y_down(tm, fm)
            if k < 2:
                ys[k, 0, a] = up
                ys[k, 1, a] = down
            else:
                ys3[0, a] = up
                ys3[1, a] = down
            start(y_copy, k, a, 2)
            return 0
        lax.fori_loop(0, count, traces_y, 0)

        def pass_z(a, _):
            traces, sums = line([u[a, 0:count, n] for n in range(MODES)], half_coef[None])
            tp, tm, fp, fm = traces
            out = spread(traces, (prev_z(tp), prev_z(fp)), (next_z(tm), next_z(fm)),
                         geom(2), c[None], sums, count)
            for n in range(count):
                acc[a, 0:count, n] = out[n]
            return 0
        lax.fori_loop(0, count, pass_z, 0)

        def pass_y(a, _):
            arrive(y_copy, k, a, 2)
            traces, sums = line([u[a, n, 0:count] for n in range(MODES)], half_coef[None])
            tp, tm, fp, fm = traces
            g_prev = yg[k, 0, a] if k < 2 else yg3[0, a]
            g_next = yg[k, 1, a] if k < 2 else yg3[1, a]
            out = spread(traces, prev_y(tp, fp, g_prev), next_y(tm, fm, g_next),
                         geom(1), c[None], sums, count)
            for n in range(count):
                acc[a, n, 0:count] += out[n]
            return 0
        lax.fori_loop(0, count, pass_y, 0)

        def pass_x(b, _, following=False):
            arrive(x_copy, k, b, 0)
            values = [u[n, b, 0:count] for n in range(MODES)]
            traces, sums = line(values, half_coef[None])
            tp, tm, fp, fm = traces
            g_prev = xg[k, 0, b] if k < 2 else xg3[0, b]
            g_next = xg[k, 1, b] if k < 2 else xg3[1, b]
            out = spread(traces, prev_x(tp, fp, g_prev), next_x(tm, fm, g_next),
                         geom(0), c[None], sums, count)
            if k < 2:
                fresh = []
                for n in range(MODES):
                    residual = s[n, b] - (acc[n, b] + out[n])
                    change = pairs[k][0] * step[n, b] + pairs[k][1] * (inv[n, b] * residual)
                    moved = values[n] + change
                    if k < 1:
                        step[n, b] = change
                    u[n, b] = moved
                    fresh.append(moved)
                if following:
                    width = MODES if k < 1 else CMODES
                    send_x(k + 1, b, [v[0:width] for v in fresh])
            else:
                low = lax.broadcasted_iota(jnp.int32, (CMODES, 8, 128), 0)
                inside_z = jnp.where(low <= (deg[2] >> 1)[None], 1.0, 0.0)
                inside_y = jnp.where((deg[1] >> 1) >= b, 1.0, 0.0)
                mass = (1.0 / ((2.0 * low.astype(F32) + 1.0) * (2.0 * b.astype(F32) + 1.0))) * (
                    inside_z * inside_y[None])
                for n in range(CMODES):
                    inside = jnp.where((deg[0] >> 1) >= n, 8.0 / (2.0 * n + 1.0), 0.0)
                    residual = s[n, b, 0:CMODES] - (acc[n, b, 0:CMODES] + out[n])
                    coarse[n, b] = residual * (mass * inside[None])
            return 0
        if k == 0:
            lax.fori_loop(0, MODES, functools.partial(pass_x, following=True), 0)
        elif k == 1:
            lax.fori_loop(0, CMODES, functools.partial(pass_x, following=True), 0)
            lax.fori_loop(CMODES, MODES, pass_x, 0)
        else:
            lax.fori_loop(0, CMODES, pass_x, 0)

    for d in range(4):
        @pl.when(exists[d])
        def _(d=d):
            param_copy(d).wait_send()
            make = (x_copy, y_copy)[d // 2]
            for k in range(3):
                def finish(i, _):
                    make(k, d % 2, i).wait_send()
                    return 0
                lax.fori_loop(0, MODES if k < 2 else CMODES, finish, 0)


def smoother(nx, ny, rhs, coef, deg):
    field = pltpu.VMEM((MODES, MODES, MODES, 8, 128), F32)
    wide = pltpu.VMEM((2, 2, MODES, MODES, 8, 128), F32)
    narrow = pltpu.VMEM((2, CMODES, CMODES, 8, 128), F32)
    return pl.pallas_call(
        functools.partial(kernel, nx, ny),
        out_shape=(jax.ShapeDtypeStruct((MODES, MODES, MODES, 8, 128), F32),
                   jax.ShapeDtypeStruct((CMODES, CMODES, CMODES, 8, 128), F32)),
        in_specs=[pl.BlockSpec(memory_space=pltpu.VMEM)] * 3,
        out_specs=[pl.BlockSpec(memory_space=pltpu.VMEM)] * 2,
        scratch_shapes=[
            field, field, field, field,
            pltpu.VMEM((3, 6, 8, 128), F32),
            pltpu.VMEM((3, MODES, 8, 128), F32),
            pltpu.VMEM((MODES, 8, 128), F32),
            pltpu.VMEM((4, 8, 128), F32),
            pltpu.VMEM((4, 8, 128), F32),
            wide, wide, wide, wide, narrow, narrow, narrow, narrow,
            pltpu.SemaphoreType.DMA((4,)),
            pltpu.SemaphoreType.DMA((4,)),
            pltpu.SemaphoreType.DMA((3, 2, MODES)),
            pltpu.SemaphoreType.DMA((3, 2, MODES)),
            pltpu.SemaphoreType.DMA((3, 2, MODES)),
            pltpu.SemaphoreType.DMA((3, 2, MODES)),
        ],
        compiler_params=pltpu.CompilerParams(
            collective_id=0, has_side_effects=True, vmem_limit_bytes=48 * 1024 * 1024
        ),
    )(rhs, coef, deg)


def solution(mesh):
    nx, ny = mesh.shape["gx"], mesh.shape["gy"]

    def body(right_side, coefficient, degrees):
        local = right_side.shape[3:]
        flat = (local[0] * local[1], local[2])
        smoothed, coarse = smoother(
            nx, ny,
            right_side.reshape(right_side.shape[:3] + flat),
            coefficient.reshape(flat),
            degrees.reshape((3,) + flat),
        )
        coarse = jnp.transpose(coarse.reshape((CMODES**3,) + local), (0, 1, 3, 2))
        folded = lax.all_to_all(coarse, "gy", split_axis=2, concat_axis=3, tiled=True)
        return (smoothed.reshape(right_side.shape),
                folded.reshape(folded.shape[0], folded.shape[1], -1))

    in_specs = (
        P(None, None, None, "gx", "gy", None),
        P("gx", "gy", None),
        P(None, "gx", "gy", None),
    )
    out_specs = (P(None, None, None, "gx", "gy", None), P(None, "gx", "gy"))
    return jax.shard_map(body, mesh=mesh, in_specs=in_specs, out_specs=out_specs, check_vma=False)
```

```python
import functools

import jax
import jax.numpy as jnp
from jax import lax
from jax.experimental import pallas as pl
from jax.experimental.pallas import tpu as pltpu
from jax.sharding import PartitionSpec as P

CMODES = 4
LAM_HIGH = 6.0
LAM_LOW = 0.5
MODES = 7
MESH = pl.DeviceIdType.MESH
F32 = jnp.float32
HALF = [(2.0 * n + 1.0) / 2.0 for n in range(MODES)]
SLOPE = [n * (n + 1.0) / 2.0 for n in range(MODES)]


def chebyshev():
    centre = (LAM_HIGH + LAM_LOW) / 2.0
    radius = (LAM_HIGH - LAM_LOW) / 2.0
    ratio = centre / radius
    rho = 1.0 / ratio
    pairs = []
    for _ in range(2):
        following = 1.0 / (2.0 * ratio - rho)
        pairs.append((following * rho, 2.0 * following / radius))
        rho = following
    return 1.0 / centre, pairs


def rows(shape):
    return lax.broadcasted_iota(jnp.int32, shape, len(shape) - 2)


def lanes(shape):
    return lax.broadcasted_iota(jnp.int32, shape, len(shape) - 1)


def turn(v, shift):
    return pltpu.roll(v, shift, v.ndim - 2)


def pack_x_up(p, q):
    return jnp.where(rows(p.shape) < 4, turn(p, 4), q)


def pack_x_down(p, q):
    return jnp.where(rows(p.shape) < 4, p, turn(q, 4))


def prev_x(p, q, g):
    low = rows(p.shape) < 4
    return jnp.where(low, g, turn(p, 4)), turn(jnp.where(low, q, g), 4)


def next_x(p, q, g):
    low = rows(p.shape) < 4
    return turn(jnp.where(low, g, p), 4), jnp.where(low, turn(q, 4), g)


def pack_y_up(p, q):
    return jnp.where((rows(p.shape) & 3) == 0, turn(p, 5), turn(q, 6))


def pack_y_down(p, q):
    return jnp.where((rows(p.shape) & 3) == 3, turn(p, 3), turn(q, 2))


def prev_y(p, q, g):
    edge = (rows(p.shape) & 3) == 0
    return jnp.where(edge, g, turn(p, 1)), jnp.where(edge, turn(g, 7), turn(q, 1))


def next_y(p, q, g):
    edge = (rows(p.shape) & 3) == 3
    return jnp.where(edge, g, turn(p, 7)), jnp.where(edge, turn(g, 1), turn(q, 7))


def prev_z(p):
    return jnp.where(lanes(p.shape) == 0, 0.0, pltpu.roll(p, 1, p.ndim - 1))


def next_z(p):
    end = p.shape[-1] - 1
    return jnp.where(lanes(p.shape) == end, 0.0, pltpu.roll(p, end, p.ndim - 1))


def line(u, half_coef):
    t4 = u[4] + u[6]
    t2 = u[2] + t4
    even = u[0] + t2
    t3 = u[3] + u[5]
    odd = u[1] + t3
    s2 = 6.0 * t2
    s4 = s2 + 14.0 * t4
    s6 = s4 + 22.0 * u[6]
    s1 = 2.0 * odd
    s3 = s1 + 10.0 * t3
    s5 = s3 + 18.0 * u[5]
    tp = even + odd
    tm = even - odd
    fp = half_coef * (s6 + s5)
    fm = half_coef * (s5 - s6)
    return (tp, tm, fp, fm), (None, s1, s2, s3, s4, s5, s6)


def spread(traces, before, after, geom, coef, sums, count):
    tp, tm, fp, fm = traces
    tau_a, tau_b, w_a, w_b, k_a, k_b = geom
    jump_a = tp - after[0]
    g_a = tau_a * jump_a - w_a * (fp + after[1])
    jump_b = before[0] - tm
    g_b = tau_b * jump_b - w_b * (before[1] + fm)
    kl = k_a * jump_a
    kr = k_b * jump_b
    p = (g_a - g_b, g_a + g_b)
    q = (kl - kr, kl + kr)
    out = [HALF[0] * p[0]]
    for n in range(1, count):
        out.append(HALF[n] * (coef * sums[n] + (p[n % 2] - SLOPE[n] * q[n % 2])))
    return out


def kernel(nx, ny, rhs_hbm, coef_hbm, deg_hbm, u, coarse, s, coef, deg, inv, step, acc, geo, dia, zm,
           ps, pg, xs, xg, ys, yg, xs3, xg3, ys3, yg3, kept, folds, folded, order,
           in_sem, p_send, p_recv, x_send, x_recv, y_send, y_recv, f_send, f_recv):
    loads = [pltpu.make_async_copy(a, b, in_sem.at[i])
             for i, (a, b) in enumerate(((coef_hbm, coef), (deg_hbm, deg), (rhs_hbm, s)))]
    for load in loads:
        load.start()
    gx, gy = lax.axis_index("gx"), lax.axis_index("gy")
    exists = (gx < nx - 1, gx > 0, gy < ny - 1, gy > 0)
    target = ({"gx": gx + 1}, {"gx": gx - 1}, {"gy": gy + 1}, {"gy": gy - 1})
    source = (exists[1], exists[0], exists[3], exists[2])

    barrier = pltpu.get_barrier_semaphore()
    for d in range(2):
        @pl.when(exists[d])
        def _(d=d):
            pl.semaphore_signal(barrier, inc=1, device_id=target[d], device_id_type=MESH)
    for d in range(ny):
        @pl.when(gy != d)
        def _(d=d):
            pl.semaphore_signal(barrier, inc=1, device_id={"gy": d}, device_id_type=MESH)

    def copy(src, dst, send, recv, d):
        return pltpu.make_async_remote_copy(src_ref=src, dst_ref=dst, send_sem=send, recv_sem=recv,
                                            device_id=target[d], device_id_type=MESH)

    def param_copy(d):
        return copy(ps.at[d], pg.at[d], p_send.at[d], p_recv.at[d], d)

    def x_copy(k, d, b):
        if k < 2:
            return copy(xs.at[k, d, b], xg.at[k, d, b], x_send.at[k, d, b], x_recv.at[k, d, b], d)
        return copy(xs3.at[d, b], xg3.at[d, b], x_send.at[k, d, b], x_recv.at[k, d, b], d)

    def y_copy(k, d, a):
        if k < 2:
            return copy(ys.at[k, d, a], yg.at[k, d, a], y_send.at[k, d, a], y_recv.at[k, d, a], 2 + d)
        return copy(ys3.at[d, a], yg3.at[d, a], y_send.at[k, d, a], y_recv.at[k, d, a], 2 + d)

    loads[0].wait()
    loads[1].wait()
    c = coef[...]
    half_coef = 0.5 * c
    df = [deg[d].astype(F32) for d in range(3)]
    ps[0] = pack_x_up(c, df[0])
    ps[1] = pack_x_down(c, df[0])
    ps[2] = pack_y_up(c, df[1])
    ps[3] = pack_y_down(c, df[1])
    pl.semaphore_wait(barrier, sum(e.astype(jnp.int32) for e in exists[:2]) + (ny - 1))
    for d in range(4):
        @pl.when(exists[d])
        def _(d=d):
            param_copy(d).start()

    for d in range(4):
        @pl.when(jnp.logical_not(source[d]))
        def _(d=d):
            pg[d] = jnp.zeros((8, 128), F32)
            ghosts = (xg, yg)[d // 2]
            ghosts3 = (xg3, yg3)[d // 2]

            def clear(i, _):
                for k in range(2):
                    ghosts[k, d % 2, i] = jnp.zeros((MODES, 8, 128), F32)
                return 0
            lax.fori_loop(0, MODES, clear, 0)

            def clear3(i, _):
                ghosts3[d % 2, i] = jnp.zeros((CMODES, 8, 128), F32)
                return 0
            lax.fori_loop(0, CMODES, clear3, 0)

    shape = (MODES, 8, 128)
    levels = lax.broadcasted_iota(jnp.int32, shape, 0)
    zm[...] = jnp.where(levels <= deg[2][None], 1.0, 0.0)

    def prepare(direction, before, after, first, last):
        degree = df[direction]
        wide_a = jnp.maximum(degree, after[1])
        wide_b = jnp.maximum(degree, before[1])
        tau_a = jnp.maximum(c, after[0]) * (wide_a + 1.0) * (wide_a + 2.0)
        tau_b = jnp.maximum(c, before[0]) * (wide_b + 1.0) * (wide_b + 2.0)
        w_a = jnp.where(last, 1.0, 0.5)
        w_b = jnp.where(first, 1.0, 0.5)
        for i, value in enumerate((tau_a, tau_b, w_a, w_b, w_a * c, w_b * c)):
            geo[direction, i] = value
        rest = (1.0 - (w_a + w_b)) * c
        for n in range(MODES):
            dia[direction, n] = HALF[n] * (tau_a + tau_b + (2.0 * SLOPE[n]) * rest)

    row, lane = rows((8, 128)), lanes((8, 128))
    prepare(2, (prev_z(c), prev_z(df[2])), (next_z(c), next_z(df[2])), lane == 0, lane == 127)
    for d in range(4):
        @pl.when(source[d])
        def _(d=d):
            param_copy(d).wait_recv()
    px, py = gx * 2 + (row >> 2), gy * 4 + (row & 3)
    prepare(0, prev_x(c, df[0], pg[0]), next_x(c, df[0], pg[1]), px == 0, px == 2 * nx - 1)
    prepare(1, prev_y(c, df[1], pg[2]), next_y(c, df[1], pg[3]), py == 0, py == 4 * ny - 1)

    first_scale, pairs = chebyshev()
    odds = 2.0 * levels.astype(F32) + 1.0

    def geom(direction):
        return tuple(geo[direction, i][None] for i in range(6))

    def start(make, k, at, base):
        for d in range(2):
            @pl.when(exists[base + d])
            def _(d=d):
                make(k, d, at).start()

    def arrive(make, k, at, base):
        for d in range(2):
            @pl.when(source[base + d])
            def _(d=d):
                make(k, d, at).wait_recv()

    def send_x(k, b, values):
        (tp, tm, fp, fm), _ = line(values, half_coef[None])
        up, down = pack_x_up(tp, fp), pack_x_down(tm, fm)
        if k < 2:
            xs[k, 0, b] = up
            xs[k, 1, b] = down
        else:
            xs3[0, b] = up
            xs3[1, b] = down
        start(x_copy, k, b, 0)

    loads[2].wait()

    def setup(b, _):
        inside_y = jnp.where(deg[1] >= b, 1.0, 0.0)[None] * zm[...]
        across = dia[1, b][None] + dia[2]
        scale = odds * ((2.0 * b.astype(F32) + 1.0) / 8.0)
        fresh = []
        for a in range(MODES):
            i = jnp.where(deg[0] >= a, 1.0, 0.0)[None] * inside_y / (dia[0, a][None] + across)
            r = s[a, b] * (scale * (2.0 * a + 1.0))
            x = i * r * first_scale
            s[a, b] = r
            inv[a, b] = i
            step[a, b] = x
            u[a, b] = x
            fresh.append(x)
        send_x(0, b, fresh)
        return 0
    lax.fori_loop(0, MODES, setup, 0)

    source_lane = lax.broadcasted_iota(jnp.int32, (128, 512), 0)
    fine_lane = lax.broadcasted_iota(jnp.int32, (128, 512), 1)
    depth = 128 // ny
    spot = (source_lane % depth) * (4 * ny) + source_lane // depth
    for d in range(ny):
        order[d] = jnp.where((source_lane < 4 * depth) & (fine_lane == spot + 4 * d), 1.0, 0.0).astype(jnp.bfloat16)

    for k in range(3):
        count = MODES if k < 2 else CMODES

        def traces_y(a, _):
            (tp, tm, fp, fm), _ = line([u[a, n, 0:count] for n in range(MODES)], half_coef[None])
            up, down = pack_y_up(tp, fp), pack_y_down(tm, fm)
            if k < 2:
                ys[k, 0, a] = up
                ys[k, 1, a] = down
            else:
                ys3[0, a] = up
                ys3[1, a] = down
            start(y_copy, k, a, 2)
            return 0
        lax.fori_loop(0, count, traces_y, 0)

        def pass_z(a, _):
            traces, sums = line([u[a, 0:count, n] for n in range(MODES)], half_coef[None])
            tp, tm, fp, fm = traces
            out = spread(traces, (prev_z(tp), prev_z(fp)), (next_z(tm), next_z(fm)),
                         geom(2), c[None], sums, count)
            for n in range(count):
                acc[a, 0:count, n] = out[n]
            return 0
        lax.fori_loop(0, count, pass_z, 0)

        def pass_y(a, _):
            arrive(y_copy, k, a, 2)
            traces, sums = line([u[a, n, 0:count] for n in range(MODES)], half_coef[None])
            tp, tm, fp, fm = traces
            g_prev = yg[k, 0, a] if k < 2 else yg3[0, a]
            g_next = yg[k, 1, a] if k < 2 else yg3[1, a]
            out = spread(traces, prev_y(tp, fp, g_prev), next_y(tm, fm, g_next),
                         geom(1), c[None], sums, count)
            for n in range(count):
                acc[a, n, 0:count] += out[n]
            return 0
        lax.fori_loop(0, count, pass_y, 0)

        def pass_x(b, _, following=False):
            arrive(x_copy, k, b, 0)
            values = [u[n, b, 0:count] for n in range(MODES)]
            traces, sums = line(values, half_coef[None])
            tp, tm, fp, fm = traces
            g_prev = xg[k, 0, b] if k < 2 else xg3[0, b]
            g_next = xg[k, 1, b] if k < 2 else xg3[1, b]
            out = spread(traces, prev_x(tp, fp, g_prev), next_x(tm, fm, g_next),
                         geom(0), c[None], sums, count)
            if k < 2:
                fresh = []
                for n in range(MODES):
                    residual = s[n, b] - (acc[n, b] + out[n])
                    change = pairs[k][0] * step[n, b] + pairs[k][1] * (inv[n, b] * residual)
                    moved = values[n] + change
                    if k < 1:
                        step[n, b] = change
                    u[n, b] = moved
                    fresh.append(moved)
                if following:
                    width = MODES if k < 1 else CMODES
                    send_x(k + 1, b, [v[0:width] for v in fresh])
            else:
                low = lax.broadcasted_iota(jnp.int32, (CMODES, 8, 128), 0)
                inside_z = jnp.where(low <= (deg[2] >> 1)[None], 1.0, 0.0)
                inside_y = jnp.where((deg[1] >> 1) >= b, 1.0, 0.0)
                mass = (1.0 / ((2.0 * low.astype(F32) + 1.0) * (2.0 * b.astype(F32) + 1.0))) * (
                    inside_z * inside_y[None])
                for n in range(CMODES):
                    inside = jnp.where((deg[0] >> 1) >= n, 8.0 / (2.0 * n + 1.0), 0.0)
                    residual = s[n, b, 0:CMODES] - (acc[n, b, 0:CMODES] + out[n])
                    kept[n, b] = residual * (mass * inside[None])
            return 0
        if k == 0:
            lax.fori_loop(0, MODES, functools.partial(pass_x, following=True), 0)
        elif k == 1:
            lax.fori_loop(0, CMODES, functools.partial(pass_x, following=True), 0)
            lax.fori_loop(CMODES, MODES, pass_x, 0)
        else:
            lax.fori_loop(0, CMODES, pass_x, 0)

    def fold_copy(d):
        return pltpu.make_async_remote_copy(
            src_ref=folds.at[d], dst_ref=folded.at[gy], send_sem=f_send.at[d], recv_sem=f_recv.at[gy],
            device_id={"gy": d}, device_id_type=MESH)

    def fold_arrival(d):
        return pltpu.make_async_remote_copy(
            src_ref=folds.at[d], dst_ref=folded.at[d], send_sem=f_send.at[d], recv_sem=f_recv.at[d],
            device_id={"gy": d}, device_id_type=MESH)

    cells = kept.reshape(CMODES**3 * 8, 128)
    block = lanes((CMODES**3, 128)) // depth
    for x in range(2):
        by_y = [cells[pl.ds(x * 4 + y, CMODES**3, stride=8), :] for y in range(4)]
        for d in range(ny):
            out = jnp.zeros((CMODES**3, 128), F32)
            for y in range(4):
                shift = ((y - d) * depth) % 128
                out = jnp.where(block == y, pltpu.roll(by_y[y], shift, 1) if shift else by_y[y], out)
            folds[d, x] = out
    for d in range(ny):
        @pl.when(gy != d)
        def _(d=d):
            fold_copy(d).start()

        @pl.when(gy == d)
        def _(d=d):
            folded[d] = folds[d]
    for d in range(ny):
        @pl.when(gy != d)
        def _(d=d):
            fold_arrival(d).wait_recv()
    total = jnp.zeros((2 * CMODES**3, 512), F32)
    for d in range(ny):
        left = folded[d].reshape(2 * CMODES**3, 128)
        for part in range(3):
            piece = left.astype(jnp.bfloat16)
            total = total + jnp.dot(piece, order[d], preferred_element_type=F32)
            if part < 2:
                left = left - piece.astype(F32)
    for x in range(2):
        for j in range(4):
            coarse[pl.ds(j * 2 + x, CMODES**3, stride=8), :] = total[
                x * CMODES**3:(x + 1) * CMODES**3, j * 128:(j + 1) * 128]
    for d in range(ny):
        @pl.when(gy != d)
        def _(d=d):
            fold_copy(d).wait_send()

    for d in range(4):
        @pl.when(exists[d])
        def _(d=d):
            param_copy(d).wait_send()
            make = (x_copy, y_copy)[d // 2]
            for k in range(3):
                def finish(i, _):
                    make(k, d % 2, i).wait_send()
                    return 0
                lax.fori_loop(0, MODES if k < 2 else CMODES, finish, 0)


def smoother(nx, ny, rhs, coef, deg):
    field = pltpu.VMEM((MODES, MODES, MODES, 8, 128), F32)
    wide = pltpu.VMEM((2, 2, MODES, MODES, 8, 128), F32)
    narrow = pltpu.VMEM((2, CMODES, CMODES, 8, 128), F32)
    return pl.pallas_call(
        functools.partial(kernel, nx, ny),
        out_shape=(jax.ShapeDtypeStruct((MODES, MODES, MODES, 8, 128), F32),
                   jax.ShapeDtypeStruct((CMODES**3 * 8, 128), F32)),
        in_specs=[pl.BlockSpec(memory_space=pltpu.HBM)] * 3,
        out_specs=[pl.BlockSpec(memory_space=pltpu.VMEM)] * 2,
        scratch_shapes=[
            field,
            pltpu.VMEM((8, 128), F32),
            pltpu.VMEM((3, 8, 128), jnp.int32),
            field, field, field,
            pltpu.VMEM((3, 6, 8, 128), F32),
            pltpu.VMEM((3, MODES, 8, 128), F32),
            pltpu.VMEM((MODES, 8, 128), F32),
            pltpu.VMEM((4, 8, 128), F32),
            pltpu.VMEM((4, 8, 128), F32),
            wide, wide, wide, wide, narrow, narrow, narrow, narrow,
            pltpu.VMEM((CMODES, CMODES, CMODES, 8, 128), F32),
            pltpu.VMEM((ny, 2, CMODES**3, 128), F32),
            pltpu.VMEM((ny, 2, CMODES**3, 128), F32),
            pltpu.VMEM((ny, 128, 512), jnp.bfloat16),
            pltpu.SemaphoreType.DMA((3,)),
            pltpu.SemaphoreType.DMA((4,)),
            pltpu.SemaphoreType.DMA((4,)),
            pltpu.SemaphoreType.DMA((3, 2, MODES)),
            pltpu.SemaphoreType.DMA((3, 2, MODES)),
            pltpu.SemaphoreType.DMA((3, 2, MODES)),
            pltpu.SemaphoreType.DMA((3, 2, MODES)),
            pltpu.SemaphoreType.DMA((ny,)),
            pltpu.SemaphoreType.DMA((ny,)),
        ],
        compiler_params=pltpu.CompilerParams(
            collective_id=0, has_side_effects=True, vmem_limit_bytes=48 * 1024 * 1024
        ),
    )(rhs, coef, deg)


def solution(mesh):
    nx, ny = mesh.shape["gx"], mesh.shape["gy"]

    def body(right_side, coefficient, degrees):
        local = right_side.shape[3:]
        flat = (local[0] * local[1], local[2])
        smoothed, coarse = smoother(
            nx, ny,
            right_side.reshape(right_side.shape[:3] + flat),
            coefficient.reshape(flat),
            degrees.reshape((3,) + flat),
        )
        coarse = jnp.transpose(coarse.reshape(CMODES**3, 4, 2, 128), (0, 2, 1, 3))
        return smoothed.reshape(right_side.shape), coarse.reshape(CMODES**3, 2, 512)

    in_specs = (
        P(None, None, None, "gx", "gy", None),
        P("gx", "gy", None),
        P(None, "gx", "gy", None),
    )
    out_specs = (P(None, None, None, "gx", "gy", None), P(None, "gx", "gy"))
    return jax.shard_map(body, mesh=mesh, in_specs=in_specs, out_specs=out_specs, check_vma=False)
```

```python
import functools

import jax
import jax.numpy as jnp
from jax import lax
from jax.experimental import pallas as pl
from jax.experimental.pallas import tpu as pltpu
from jax.sharding import PartitionSpec as P

CMODES = 4
LAM_HIGH = 6.0
LAM_LOW = 0.5
MODES = 7
MESH = pl.DeviceIdType.MESH
F32 = jnp.float32
HALF = [(2.0 * n + 1.0) / 2.0 for n in range(MODES)]
SLOPE = [n * (n + 1.0) / 2.0 for n in range(MODES)]


def chebyshev():
    centre = (LAM_HIGH + LAM_LOW) / 2.0
    radius = (LAM_HIGH - LAM_LOW) / 2.0
    ratio = centre / radius
    rho = 1.0 / ratio
    pairs = []
    for _ in range(2):
        following = 1.0 / (2.0 * ratio - rho)
        pairs.append((following * rho, 2.0 * following / radius))
        rho = following
    return 1.0 / centre, pairs


def rows(shape):
    return lax.broadcasted_iota(jnp.int32, shape, len(shape) - 2)


def lanes(shape):
    return lax.broadcasted_iota(jnp.int32, shape, len(shape) - 1)


def turn(v, shift):
    return pltpu.roll(v, shift, v.ndim - 2)


def pack_x_up(p, q):
    return jnp.where(rows(p.shape) < 4, turn(p, 4), q)


def pack_x_down(p, q):
    return jnp.where(rows(p.shape) < 4, p, turn(q, 4))


def prev_x(p, q, g):
    low = rows(p.shape) < 4
    return jnp.where(low, g, turn(p, 4)), turn(jnp.where(low, q, g), 4)


def next_x(p, q, g):
    low = rows(p.shape) < 4
    return turn(jnp.where(low, g, p), 4), jnp.where(low, turn(q, 4), g)


def pack_y_up(p, q):
    return jnp.where((rows(p.shape) & 3) == 0, turn(p, 5), turn(q, 6))


def pack_y_down(p, q):
    return jnp.where((rows(p.shape) & 3) == 3, turn(p, 3), turn(q, 2))


def prev_y(p, q, g):
    edge = (rows(p.shape) & 3) == 0
    return jnp.where(edge, g, turn(p, 1)), jnp.where(edge, turn(g, 7), turn(q, 1))


def next_y(p, q, g):
    edge = (rows(p.shape) & 3) == 3
    return jnp.where(edge, g, turn(p, 7)), jnp.where(edge, turn(g, 1), turn(q, 7))


def prev_z(p):
    return jnp.where(lanes(p.shape) == 0, 0.0, pltpu.roll(p, 1, p.ndim - 1))


def next_z(p):
    end = p.shape[-1] - 1
    return jnp.where(lanes(p.shape) == end, 0.0, pltpu.roll(p, end, p.ndim - 1))


def line(u, half_coef):
    t4 = u[4] + u[6]
    t2 = u[2] + t4
    even = u[0] + t2
    t3 = u[3] + u[5]
    odd = u[1] + t3
    s2 = 6.0 * t2
    s4 = s2 + 14.0 * t4
    s6 = s4 + 22.0 * u[6]
    s1 = 2.0 * odd
    s3 = s1 + 10.0 * t3
    s5 = s3 + 18.0 * u[5]
    tp = even + odd
    tm = even - odd
    fp = half_coef * (s6 + s5)
    fm = half_coef * (s5 - s6)
    return (tp, tm, fp, fm), (None, s1, s2, s3, s4, s5, s6)


def spread(traces, before, after, geom, coef, sums, count):
    tp, tm, fp, fm = traces
    tau_a, tau_b, w_a, w_b, k_a, k_b = geom
    jump_a = tp - after[0]
    g_a = tau_a * jump_a - w_a * (fp + after[1])
    jump_b = before[0] - tm
    g_b = tau_b * jump_b - w_b * (before[1] + fm)
    kl = k_a * jump_a
    kr = k_b * jump_b
    p = (g_a - g_b, g_a + g_b)
    q = (kl - kr, kl + kr)
    out = [HALF[0] * p[0]]
    for n in range(1, count):
        out.append(HALF[n] * (coef * sums[n] + (p[n % 2] - SLOPE[n] * q[n % 2])))
    return out


def kernel(nx, ny, rhs_hbm, coef_hbm, deg_hbm, u, coarse, s, coef, deg, inv, step, acc, geo, dia, zm,
           ps, pg, xs, xg, ys, yg, xs3, xg3, ys3, yg3, kept, folds, folded, order,
           in_sem, p_send, p_recv, x_send, x_recv, y_send, y_recv, f_send, f_recv):
    loads = [pltpu.make_async_copy(a, b, in_sem.at[i])
             for i, (a, b) in enumerate(((coef_hbm, coef), (deg_hbm, deg), (rhs_hbm, s)))]
    for load in loads:
        load.start()
    gx, gy = lax.axis_index("gx"), lax.axis_index("gy")
    exists = (gx < nx - 1, gx > 0, gy < ny - 1, gy > 0)
    target = ({"gx": gx + 1}, {"gx": gx - 1}, {"gy": gy + 1}, {"gy": gy - 1})
    source = (exists[1], exists[0], exists[3], exists[2])

    barrier = pltpu.get_barrier_semaphore()
    for d in range(2):
        @pl.when(exists[d])
        def _(d=d):
            pl.semaphore_signal(barrier, inc=1, device_id=target[d], device_id_type=MESH)
    for d in range(ny):
        @pl.when(gy != d)
        def _(d=d):
            pl.semaphore_signal(barrier, inc=1, device_id={"gy": d}, device_id_type=MESH)

    def copy(src, dst, send, recv, d):
        return pltpu.make_async_remote_copy(src_ref=src, dst_ref=dst, send_sem=send, recv_sem=recv,
                                            device_id=target[d], device_id_type=MESH)

    def param_copy(d):
        return copy(ps.at[d], pg.at[d], p_send.at[d], p_recv.at[d], d)

    def x_copy(k, d, b):
        if k < 2:
            return copy(xs.at[k, d, b], xg.at[k, d, b], x_send.at[k, d, b], x_recv.at[k, d, b], d)
        return copy(xs3.at[d, b], xg3.at[d, b], x_send.at[k, d, b], x_recv.at[k, d, b], d)

    def y_copy(k, d, a):
        if k < 2:
            return copy(ys.at[k, d, a], yg.at[k, d, a], y_send.at[k, d, a], y_recv.at[k, d, a], 2 + d)
        return copy(ys3.at[d, a], yg3.at[d, a], y_send.at[k, d, a], y_recv.at[k, d, a], 2 + d)

    loads[0].wait()
    loads[1].wait()
    c = coef[...]
    half_coef = 0.5 * c
    depth = 128 // ny
    df = [deg[d].astype(F32) for d in range(3)]
    ps[0] = pack_x_up(c, df[0])
    ps[1] = pack_x_down(c, df[0])
    ps[2] = pack_y_up(c, df[1])
    ps[3] = pack_y_down(c, df[1])
    pl.semaphore_wait(barrier, sum(e.astype(jnp.int32) for e in exists[:2]) + (ny - 1))
    for d in range(4):
        @pl.when(exists[d])
        def _(d=d):
            param_copy(d).start()

    source_lane = lax.broadcasted_iota(jnp.int32, (128, 512), 0)
    fine_lane = lax.broadcasted_iota(jnp.int32, (128, 512), 1)
    spot = (source_lane % depth) * (4 * ny) + source_lane // depth
    for d in range(ny):
        order[d * 128:(d + 1) * 128] = jnp.where((source_lane < 4 * depth) & (fine_lane == spot + 4 * d), 1.0, 0.0).astype(jnp.bfloat16)

    for d in range(4):
        @pl.when(jnp.logical_not(source[d]))
        def _(d=d):
            pg[d] = jnp.zeros((8, 128), F32)
            ghosts = (xg, yg)[d // 2]
            ghosts3 = (xg3, yg3)[d // 2]

            def clear(i, _):
                for k in range(2):
                    ghosts[k, d % 2, i] = jnp.zeros((MODES, 8, 128), F32)
                return 0
            lax.fori_loop(0, MODES, clear, 0)

            def clear3(i, _):
                ghosts3[d % 2, i] = jnp.zeros((CMODES, 8, 128), F32)
                return 0
            lax.fori_loop(0, CMODES, clear3, 0)

    shape = (MODES, 8, 128)
    levels = lax.broadcasted_iota(jnp.int32, shape, 0)
    zm[...] = jnp.where(levels <= deg[2][None], 1.0, 0.0)

    def prepare(direction, before, after, first, last):
        degree = df[direction]
        wide_a = jnp.maximum(degree, after[1])
        wide_b = jnp.maximum(degree, before[1])
        tau_a = jnp.maximum(c, after[0]) * (wide_a + 1.0) * (wide_a + 2.0)
        tau_b = jnp.maximum(c, before[0]) * (wide_b + 1.0) * (wide_b + 2.0)
        w_a = jnp.where(last, 1.0, 0.5)
        w_b = jnp.where(first, 1.0, 0.5)
        for i, value in enumerate((tau_a, tau_b, w_a, w_b, w_a * c, w_b * c)):
            geo[direction, i] = value
        rest = (1.0 - (w_a + w_b)) * c
        for n in range(MODES):
            dia[direction, n] = HALF[n] * (tau_a + tau_b + (2.0 * SLOPE[n]) * rest)

    row, lane = rows((8, 128)), lanes((8, 128))
    prepare(2, (prev_z(c), prev_z(df[2])), (next_z(c), next_z(df[2])), lane == 0, lane == 127)
    for d in range(4):
        @pl.when(source[d])
        def _(d=d):
            param_copy(d).wait_recv()
    px, py = gx * 2 + (row >> 2), gy * 4 + (row & 3)
    prepare(0, prev_x(c, df[0], pg[0]), next_x(c, df[0], pg[1]), px == 0, px == 2 * nx - 1)
    prepare(1, prev_y(c, df[1], pg[2]), next_y(c, df[1], pg[3]), py == 0, py == 4 * ny - 1)

    first_scale, pairs = chebyshev()
    odds = 2.0 * levels.astype(F32) + 1.0

    def geom(direction):
        return tuple(geo[direction, i][None] for i in range(6))

    def start(make, k, at, base):
        for d in range(2):
            @pl.when(exists[base + d])
            def _(d=d):
                make(k, d, at).start()

    def arrive(make, k, at, base):
        for d in range(2):
            @pl.when(source[base + d])
            def _(d=d):
                make(k, d, at).wait_recv()

    def send_x(k, b, values):
        (tp, tm, fp, fm), _ = line(values, half_coef[None])
        up, down = pack_x_up(tp, fp), pack_x_down(tm, fm)
        if k < 2:
            xs[k, 0, b] = up
            xs[k, 1, b] = down
        else:
            xs3[0, b] = up
            xs3[1, b] = down
        start(x_copy, k, b, 0)

    loads[2].wait()

    def setup(b, _):
        inside_y = jnp.where(deg[1] >= b, 1.0, 0.0)[None] * zm[...]
        across = dia[1, b][None] + dia[2]
        scale = odds * ((2.0 * b.astype(F32) + 1.0) / 8.0)
        fresh = []
        for a in range(MODES):
            i = jnp.where(deg[0] >= a, 1.0, 0.0)[None] * inside_y / (dia[0, a][None] + across)
            r = s[a, b] * (scale * (2.0 * a + 1.0))
            x = i * r * first_scale
            s[a, b] = r
            inv[a, b] = i
            step[a, b] = x
            u[a, b] = x
            fresh.append(x)
        send_x(0, b, fresh)
        return 0
    lax.fori_loop(0, MODES, setup, 0)

    def fold_copy(d, b):
        return pltpu.make_async_remote_copy(
            src_ref=folds.at[d, b], dst_ref=folded.at[gy, b], send_sem=f_send.at[d, b],
            recv_sem=f_recv.at[gy, b], device_id={"gy": d}, device_id_type=MESH)

    def fold_arrival(d, b):
        return pltpu.make_async_remote_copy(
            src_ref=folds.at[d, b], dst_ref=folded.at[d, b], send_sem=f_send.at[d, b],
            recv_sem=f_recv.at[d, b], device_id={"gy": d}, device_id_type=MESH)

    def fold(b):
        block = lanes((CMODES**2, 128)) // depth
        for x in range(2):
            by_y = [kept[b, pl.ds(x * 4 + y, CMODES**2, stride=8), :] for y in range(4)]
            for d in range(ny):
                out = jnp.zeros((CMODES**2, 128), F32)
                for y in range(4):
                    shift = ((y - d) * depth) % 128
                    out = jnp.where(block == y, pltpu.roll(by_y[y], shift, 1) if shift else by_y[y], out)
                folds[d, b, x] = out
        for d in range(ny):
            @pl.when(gy != d)
            def _(d=d):
                fold_copy(d, b).start()

            @pl.when(gy == d)
            def _(d=d):
                folded[d, b] = folds[d, b]

    for k in range(3):
        count = MODES if k < 2 else CMODES

        def traces_y(a, _):
            (tp, tm, fp, fm), _ = line([u[a, n, 0:count] for n in range(MODES)], half_coef[None])
            up, down = pack_y_up(tp, fp), pack_y_down(tm, fm)
            if k < 2:
                ys[k, 0, a] = up
                ys[k, 1, a] = down
            else:
                ys3[0, a] = up
                ys3[1, a] = down
            start(y_copy, k, a, 2)
            return 0
        lax.fori_loop(0, count, traces_y, 0)

        def pass_z(a, _):
            traces, sums = line([u[a, 0:count, n] for n in range(MODES)], half_coef[None])
            tp, tm, fp, fm = traces
            out = spread(traces, (prev_z(tp), prev_z(fp)), (next_z(tm), next_z(fm)),
                         geom(2), c[None], sums, count)
            for n in range(count):
                acc[a, 0:count, n] = out[n]
            return 0
        lax.fori_loop(0, count, pass_z, 0)

        def pass_y(a, _):
            arrive(y_copy, k, a, 2)
            traces, sums = line([u[a, n, 0:count] for n in range(MODES)], half_coef[None])
            tp, tm, fp, fm = traces
            g_prev = yg[k, 0, a] if k < 2 else yg3[0, a]
            g_next = yg[k, 1, a] if k < 2 else yg3[1, a]
            out = spread(traces, prev_y(tp, fp, g_prev), next_y(tm, fm, g_next),
                         geom(1), c[None], sums, count)
            for n in range(count):
                acc[a, n, 0:count] += out[n]
            return 0
        lax.fori_loop(0, count, pass_y, 0)

        def pass_x(b, _, following=False):
            arrive(x_copy, k, b, 0)
            values = [u[n, b, 0:count] for n in range(MODES)]
            traces, sums = line(values, half_coef[None])
            tp, tm, fp, fm = traces
            g_prev = xg[k, 0, b] if k < 2 else xg3[0, b]
            g_next = xg[k, 1, b] if k < 2 else xg3[1, b]
            out = spread(traces, prev_x(tp, fp, g_prev), next_x(tm, fm, g_next),
                         geom(0), c[None], sums, count)
            if k < 2:
                fresh = []
                for n in range(MODES):
                    residual = s[n, b] - (acc[n, b] + out[n])
                    change = pairs[k][0] * step[n, b] + pairs[k][1] * (inv[n, b] * residual)
                    moved = values[n] + change
                    if k < 1:
                        step[n, b] = change
                    u[n, b] = moved
                    fresh.append(moved)
                if following:
                    width = MODES if k < 1 else CMODES
                    send_x(k + 1, b, [v[0:width] for v in fresh])
            else:
                low = lax.broadcasted_iota(jnp.int32, (CMODES, 8, 128), 0)
                inside_z = jnp.where(low <= (deg[2] >> 1)[None], 1.0, 0.0)
                inside_y = jnp.where((deg[1] >> 1) >= b, 1.0, 0.0)
                mass = (1.0 / ((2.0 * low.astype(F32) + 1.0) * (2.0 * b.astype(F32) + 1.0))) * (
                    inside_z * inside_y[None])
                for n in range(CMODES):
                    inside = jnp.where((deg[0] >> 1) >= n, 8.0 / (2.0 * n + 1.0), 0.0)
                    residual = s[n, b, 0:CMODES] - (acc[n, b, 0:CMODES] + out[n])
                    kept[b, n * 32:(n + 1) * 32] = (residual * (mass * inside[None])).reshape(32, 128)
                fold(b)
            return 0
        if k == 0:
            lax.fori_loop(0, MODES, functools.partial(pass_x, following=True), 0)
        elif k == 1:
            lax.fori_loop(0, CMODES, functools.partial(pass_x, following=True), 0)
            lax.fori_loop(CMODES, MODES, pass_x, 0)
        else:
            lax.fori_loop(0, CMODES, pass_x, 0)

    for d in range(ny):
        @pl.when(gy != d)
        def _(d=d):
            for b in range(CMODES):
                fold_arrival(d, b).wait_recv()
    left = jnp.concatenate([folded[d].reshape(2 * CMODES**3, 128) for d in range(ny)], axis=1)
    total = jnp.zeros((2 * CMODES**3, 512), F32)
    for part in range(3):
        piece = left.astype(jnp.bfloat16)
        total = total + jnp.dot(piece, order[...], preferred_element_type=F32)
        if part < 2:
            left = left - piece.astype(F32)
    for b in range(CMODES):
        for x in range(2):
            for n in range(CMODES):
                for j in range(4):
                    coarse[pl.ds((n * 16 + b * 4) * 8 + j * 2 + x, CMODES, stride=8), :] = total[
                        b * 32 + x * 16 + n * 4:b * 32 + x * 16 + n * 4 + 4, j * 128:(j + 1) * 128]
    for d in range(ny):
        @pl.when(gy != d)
        def _(d=d):
            for b in range(CMODES):
                fold_copy(d, b).wait_send()

    for d in range(4):
        @pl.when(exists[d])
        def _(d=d):
            param_copy(d).wait_send()
            make = (x_copy, y_copy)[d // 2]
            for k in range(3):
                def finish(i, _):
                    make(k, d % 2, i).wait_send()
                    return 0
                lax.fori_loop(0, MODES if k < 2 else CMODES, finish, 0)


def smoother(nx, ny, rhs, coef, deg):
    field = pltpu.VMEM((MODES, MODES, MODES, 8, 128), F32)
    wide = pltpu.VMEM((2, 2, MODES, MODES, 8, 128), F32)
    narrow = pltpu.VMEM((2, CMODES, CMODES, 8, 128), F32)
    return pl.pallas_call(
        functools.partial(kernel, nx, ny),
        out_shape=(jax.ShapeDtypeStruct((MODES, MODES, MODES, 8, 128), F32),
                   jax.ShapeDtypeStruct((CMODES**3 * 8, 128), F32)),
        in_specs=[pl.BlockSpec(memory_space=pltpu.HBM)] * 3,
        out_specs=[pl.BlockSpec(memory_space=pltpu.VMEM)] * 2,
        scratch_shapes=[
            field,
            pltpu.VMEM((8, 128), F32),
            pltpu.VMEM((3, 8, 128), jnp.int32),
            field, field, field,
            pltpu.VMEM((3, 6, 8, 128), F32),
            pltpu.VMEM((3, MODES, 8, 128), F32),
            pltpu.VMEM((MODES, 8, 128), F32),
            pltpu.VMEM((4, 8, 128), F32),
            pltpu.VMEM((4, 8, 128), F32),
            wide, wide, wide, wide, narrow, narrow, narrow, narrow,
            pltpu.VMEM((CMODES, 128, 128), F32),
            pltpu.VMEM((ny, CMODES, 2, CMODES**2, 128), F32),
            pltpu.VMEM((ny, CMODES, 2, CMODES**2, 128), F32),
            pltpu.VMEM((ny * 128, 512), jnp.bfloat16),
            pltpu.SemaphoreType.DMA((3,)),
            pltpu.SemaphoreType.DMA((4,)),
            pltpu.SemaphoreType.DMA((4,)),
            pltpu.SemaphoreType.DMA((3, 2, MODES)),
            pltpu.SemaphoreType.DMA((3, 2, MODES)),
            pltpu.SemaphoreType.DMA((3, 2, MODES)),
            pltpu.SemaphoreType.DMA((3, 2, MODES)),
            pltpu.SemaphoreType.DMA((ny, CMODES)),
            pltpu.SemaphoreType.DMA((ny, CMODES)),
        ],
        compiler_params=pltpu.CompilerParams(
            collective_id=0, has_side_effects=True, vmem_limit_bytes=48 * 1024 * 1024
        ),
    )(*(pltpu.with_memory_space_constraint(v, pltpu.HBM) for v in (rhs, coef, deg)))


def solution(mesh):
    nx, ny = mesh.shape["gx"], mesh.shape["gy"]

    def body(right_side, coefficient, degrees):
        local = right_side.shape[3:]
        flat = (local[0] * local[1], local[2])
        smoothed, coarse = smoother(
            nx, ny,
            right_side.reshape(right_side.shape[:3] + flat),
            coefficient.reshape(flat),
            degrees.reshape((3,) + flat),
        )
        coarse = jnp.transpose(coarse.reshape(CMODES**3, 4, 2, 128), (0, 2, 1, 3))
        return smoothed.reshape(right_side.shape), coarse.reshape(CMODES**3, 2, 512)

    in_specs = (
        P(None, None, None, "gx", "gy", None),
        P("gx", "gy", None),
        P(None, "gx", "gy", None),
    )
    out_specs = (P(None, None, None, "gx", "gy", None), P(None, "gx", "gy"))
    return jax.shard_map(body, mesh=mesh, in_specs=in_specs, out_specs=out_specs, check_vma=False)
```

```python
import functools

import jax
import jax.numpy as jnp
from jax import lax
from jax.experimental import pallas as pl
from jax.experimental.pallas import tpu as pltpu
from jax.sharding import PartitionSpec as P

CMODES = 4
LAM_HIGH = 6.0
LAM_LOW = 0.5
MODES = 7
MESH = pl.DeviceIdType.MESH
F32 = jnp.float32
HALF = [(2.0 * n + 1.0) / 2.0 for n in range(MODES)]
SLOPE = [n * (n + 1.0) / 2.0 for n in range(MODES)]


def chebyshev():
    centre = (LAM_HIGH + LAM_LOW) / 2.0
    radius = (LAM_HIGH - LAM_LOW) / 2.0
    ratio = centre / radius
    rho = 1.0 / ratio
    pairs = []
    for _ in range(2):
        following = 1.0 / (2.0 * ratio - rho)
        pairs.append((following * rho, 2.0 * following / radius))
        rho = following
    return 1.0 / centre, pairs


def rows(shape):
    return lax.broadcasted_iota(jnp.int32, shape, len(shape) - 2)


def lanes(shape):
    return lax.broadcasted_iota(jnp.int32, shape, len(shape) - 1)


def turn(v, shift):
    return pltpu.roll(v, shift, v.ndim - 2)


def pack_x_up(p, q):
    return jnp.where(rows(p.shape) < 4, turn(p, 4), q)


def pack_x_down(p, q):
    return jnp.where(rows(p.shape) < 4, p, turn(q, 4))


def prev_x(p, q, g):
    low = rows(p.shape) < 4
    return jnp.where(low, g, turn(p, 4)), turn(jnp.where(low, q, g), 4)


def next_x(p, q, g):
    low = rows(p.shape) < 4
    return turn(jnp.where(low, g, p), 4), jnp.where(low, turn(q, 4), g)


def pack_y_up(p, q):
    return jnp.where((rows(p.shape) & 3) == 0, turn(p, 5), turn(q, 6))


def pack_y_down(p, q):
    return jnp.where((rows(p.shape) & 3) == 3, turn(p, 3), turn(q, 2))


def prev_y(p, q, g):
    edge = (rows(p.shape) & 3) == 0
    return jnp.where(edge, g, turn(p, 1)), jnp.where(edge, turn(g, 7), turn(q, 1))


def next_y(p, q, g):
    edge = (rows(p.shape) & 3) == 3
    return jnp.where(edge, g, turn(p, 7)), jnp.where(edge, turn(g, 1), turn(q, 7))


def prev_z(p):
    return jnp.where(lanes(p.shape) == 0, 0.0, pltpu.roll(p, 1, p.ndim - 1))


def next_z(p):
    end = p.shape[-1] - 1
    return jnp.where(lanes(p.shape) == end, 0.0, pltpu.roll(p, end, p.ndim - 1))


def line(u, half_coef):
    t4 = u[4] + u[6]
    t2 = u[2] + t4
    even = u[0] + t2
    t3 = u[3] + u[5]
    odd = u[1] + t3
    s2 = 6.0 * t2
    s4 = s2 + 14.0 * t4
    s6 = s4 + 22.0 * u[6]
    s1 = 2.0 * odd
    s3 = s1 + 10.0 * t3
    s5 = s3 + 18.0 * u[5]
    tp = even + odd
    tm = even - odd
    fp = half_coef * (s6 + s5)
    fm = half_coef * (s5 - s6)
    return (tp, tm, fp, fm), (None, s1, s2, s3, s4, s5, s6)


def spread(traces, before, after, geom, coef, sums, count):
    tp, tm, fp, fm = traces
    tau_a, tau_b, w_a, w_b, k_a, k_b = geom
    jump_a = tp - after[0]
    g_a = tau_a * jump_a - w_a * (fp + after[1])
    jump_b = before[0] - tm
    g_b = tau_b * jump_b - w_b * (before[1] + fm)
    kl = k_a * jump_a
    kr = k_b * jump_b
    p = (g_a - g_b, g_a + g_b)
    q = (kl - kr, kl + kr)
    out = [HALF[0] * p[0]]
    for n in range(1, count):
        out.append(HALF[n] * (coef * sums[n] + (p[n % 2] - SLOPE[n] * q[n % 2])))
    return out


def kernel(nx, ny, rhs_hbm, coef_hbm, deg_hbm, u, left, s, coef, deg, inv, step, acc, geo, dia, zm,
           ps, pg, xs, xg, ys, yg, xs3, xg3, ys3, yg3, kept, folds, folded,
           in_sem, p_send, p_recv, x_send, x_recv, y_send, y_recv, f_send, f_recv):
    loads = [pltpu.make_async_copy(a, b, in_sem.at[i])
             for i, (a, b) in enumerate(((coef_hbm, coef), (deg_hbm, deg), (rhs_hbm, s)))]
    for load in loads:
        load.start()
    gx, gy = lax.axis_index("gx"), lax.axis_index("gy")
    exists = (gx < nx - 1, gx > 0, gy < ny - 1, gy > 0)
    target = ({"gx": gx + 1}, {"gx": gx - 1}, {"gy": gy + 1}, {"gy": gy - 1})
    source = (exists[1], exists[0], exists[3], exists[2])

    barrier = pltpu.get_barrier_semaphore()
    for d in range(2):
        @pl.when(exists[d])
        def _(d=d):
            pl.semaphore_signal(barrier, inc=1, device_id=target[d], device_id_type=MESH)
    for d in range(ny):
        @pl.when(gy != d)
        def _(d=d):
            pl.semaphore_signal(barrier, inc=1, device_id={"gy": d}, device_id_type=MESH)

    def copy(src, dst, send, recv, d):
        return pltpu.make_async_remote_copy(src_ref=src, dst_ref=dst, send_sem=send, recv_sem=recv,
                                            device_id=target[d], device_id_type=MESH)

    def param_copy(d):
        return copy(ps.at[d], pg.at[d], p_send.at[d], p_recv.at[d], d)

    def x_copy(k, d, b):
        if k < 2:
            return copy(xs.at[k, d, b], xg.at[k, d, b], x_send.at[k, d, b], x_recv.at[k, d, b], d)
        return copy(xs3.at[d, b], xg3.at[d, b], x_send.at[k, d, b], x_recv.at[k, d, b], d)

    def y_copy(k, d, a):
        if k < 2:
            return copy(ys.at[k, d, a], yg.at[k, d, a], y_send.at[k, d, a], y_recv.at[k, d, a], 2 + d)
        return copy(ys3.at[d, a], yg3.at[d, a], y_send.at[k, d, a], y_recv.at[k, d, a], 2 + d)

    loads[0].wait()
    loads[1].wait()
    c = coef[...]
    half_coef = 0.5 * c
    depth = 128 // ny
    df = [deg[d].astype(F32) for d in range(3)]
    ps[0] = pack_x_up(c, df[0])
    ps[1] = pack_x_down(c, df[0])
    ps[2] = pack_y_up(c, df[1])
    ps[3] = pack_y_down(c, df[1])
    pl.semaphore_wait(barrier, sum(e.astype(jnp.int32) for e in exists[:2]) + (ny - 1))
    for d in range(4):
        @pl.when(exists[d])
        def _(d=d):
            param_copy(d).start()

    for d in range(4):
        @pl.when(jnp.logical_not(source[d]))
        def _(d=d):
            pg[d] = jnp.zeros((8, 128), F32)
            ghosts = (xg, yg)[d // 2]
            ghosts3 = (xg3, yg3)[d // 2]

            def clear(i, _):
                for k in range(2):
                    ghosts[k, d % 2, i] = jnp.zeros((MODES, 8, 128), F32)
                return 0
            lax.fori_loop(0, MODES, clear, 0)

            def clear3(i, _):
                ghosts3[d % 2, i] = jnp.zeros((CMODES, 8, 128), F32)
                return 0
            lax.fori_loop(0, CMODES, clear3, 0)

    shape = (MODES, 8, 128)
    levels = lax.broadcasted_iota(jnp.int32, shape, 0)
    zm[...] = jnp.where(levels <= deg[2][None], 1.0, 0.0)

    def prepare(direction, before, after, first, last):
        degree = df[direction]
        wide_a = jnp.maximum(degree, after[1])
        wide_b = jnp.maximum(degree, before[1])
        tau_a = jnp.maximum(c, after[0]) * (wide_a + 1.0) * (wide_a + 2.0)
        tau_b = jnp.maximum(c, before[0]) * (wide_b + 1.0) * (wide_b + 2.0)
        w_a = jnp.where(last, 1.0, 0.5)
        w_b = jnp.where(first, 1.0, 0.5)
        for i, value in enumerate((tau_a, tau_b, w_a, w_b, w_a * c, w_b * c)):
            geo[direction, i] = value
        rest = (1.0 - (w_a + w_b)) * c
        for n in range(MODES):
            dia[direction, n] = HALF[n] * (tau_a + tau_b + (2.0 * SLOPE[n]) * rest)

    row, lane = rows((8, 128)), lanes((8, 128))
    prepare(2, (prev_z(c), prev_z(df[2])), (next_z(c), next_z(df[2])), lane == 0, lane == 127)
    for d in range(4):
        @pl.when(source[d])
        def _(d=d):
            param_copy(d).wait_recv()
    px, py = gx * 2 + (row >> 2), gy * 4 + (row & 3)
    prepare(0, prev_x(c, df[0], pg[0]), next_x(c, df[0], pg[1]), px == 0, px == 2 * nx - 1)
    prepare(1, prev_y(c, df[1], pg[2]), next_y(c, df[1], pg[3]), py == 0, py == 4 * ny - 1)

    first_scale, pairs = chebyshev()
    odds = 2.0 * levels.astype(F32) + 1.0

    def geom(direction):
        return tuple(geo[direction, i][None] for i in range(6))

    def start(make, k, at, base):
        for d in range(2):
            @pl.when(exists[base + d])
            def _(d=d):
                make(k, d, at).start()

    def arrive(make, k, at, base):
        for d in range(2):
            @pl.when(source[base + d])
            def _(d=d):
                make(k, d, at).wait_recv()

    def send_x(k, b, values):
        (tp, tm, fp, fm), _ = line(values, half_coef[None])
        up, down = pack_x_up(tp, fp), pack_x_down(tm, fm)
        if k < 2:
            xs[k, 0, b] = up
            xs[k, 1, b] = down
        else:
            xs3[0, b] = up
            xs3[1, b] = down
        start(x_copy, k, b, 0)

    loads[2].wait()

    def setup(b, _):
        inside_y = jnp.where(deg[1] >= b, 1.0, 0.0)[None] * zm[...]
        across = dia[1, b][None] + dia[2]
        scale = odds * ((2.0 * b.astype(F32) + 1.0) / 8.0)
        fresh = []
        for a in range(MODES):
            i = jnp.where(deg[0] >= a, 1.0, 0.0)[None] * inside_y / (dia[0, a][None] + across)
            r = s[a, b] * (scale * (2.0 * a + 1.0))
            x = i * r * first_scale
            s[a, b] = r
            inv[a, b] = i
            step[a, b] = x
            u[a, b] = x
            fresh.append(x)
        send_x(0, b, fresh)
        return 0
    lax.fori_loop(0, MODES, setup, 0)

    def fold_copy(d, b):
        return pltpu.make_async_remote_copy(
            src_ref=folds.at[d, b], dst_ref=folded.at[gy, b], send_sem=f_send.at[d, b],
            recv_sem=f_recv.at[gy, b], device_id={"gy": d}, device_id_type=MESH)

    def fold_arrival(d, b):
        return pltpu.make_async_remote_copy(
            src_ref=folds.at[d, b], dst_ref=folded.at[d, b], send_sem=f_send.at[d, b],
            recv_sem=f_recv.at[d, b], device_id={"gy": d}, device_id_type=MESH)

    def fold(b):
        block = lanes((CMODES**2, 128)) // depth
        for x in range(2):
            by_y = [kept[b, pl.ds(x * 4 + y, CMODES**2, stride=8), :] for y in range(4)]
            for d in range(ny):
                out = jnp.zeros((CMODES**2, 128), F32)
                for y in range(4):
                    shift = ((y - d) * depth) % 128
                    out = jnp.where(block == y, pltpu.roll(by_y[y], shift, 1) if shift else by_y[y], out)
                folds[d, b, x] = out
        for d in range(ny):
            @pl.when(gy // 2 != d // 2)
            def _(d=d):
                fold_copy(d, b).start()
        for d in range(ny):
            @pl.when((gy // 2 == d // 2) & (gy != d))
            def _(d=d):
                fold_copy(d, b).start()

            @pl.when(gy == d)
            def _(d=d):
                folded[d, b] = folds[d, b]

    for k in range(3):
        count = MODES if k < 2 else CMODES

        def traces_y(a, _):
            (tp, tm, fp, fm), _ = line([u[a, n, 0:count] for n in range(MODES)], half_coef[None])
            up, down = pack_y_up(tp, fp), pack_y_down(tm, fm)
            if k < 2:
                ys[k, 0, a] = up
                ys[k, 1, a] = down
            else:
                ys3[0, a] = up
                ys3[1, a] = down
            start(y_copy, k, a, 2)
            return 0
        lax.fori_loop(0, count, traces_y, 0)

        def pass_z(a, _):
            traces, sums = line([u[a, 0:count, n] for n in range(MODES)], half_coef[None])
            tp, tm, fp, fm = traces
            out = spread(traces, (prev_z(tp), prev_z(fp)), (next_z(tm), next_z(fm)),
                         geom(2), c[None], sums, count)
            for n in range(count):
                acc[a, 0:count, n] = out[n]
            return 0
        lax.fori_loop(0, count, pass_z, 0)

        def pass_y(a, _):
            arrive(y_copy, k, a, 2)
            traces, sums = line([u[a, n, 0:count] for n in range(MODES)], half_coef[None])
            tp, tm, fp, fm = traces
            g_prev = yg[k, 0, a] if k < 2 else yg3[0, a]
            g_next = yg[k, 1, a] if k < 2 else yg3[1, a]
            out = spread(traces, prev_y(tp, fp, g_prev), next_y(tm, fm, g_next),
                         geom(1), c[None], sums, count)
            for n in range(count):
                acc[a, n, 0:count] += out[n]
            return 0
        lax.fori_loop(0, count, pass_y, 0)

        def pass_x(b, _, following=False):
            arrive(x_copy, k, b, 0)
            values = [u[n, b, 0:count] for n in range(MODES)]
            traces, sums = line(values, half_coef[None])
            tp, tm, fp, fm = traces
            g_prev = xg[k, 0, b] if k < 2 else xg3[0, b]
            g_next = xg[k, 1, b] if k < 2 else xg3[1, b]
            out = spread(traces, prev_x(tp, fp, g_prev), next_x(tm, fm, g_next),
                         geom(0), c[None], sums, count)
            if k < 2:
                fresh = []
                for n in range(MODES):
                    residual = s[n, b] - (acc[n, b] + out[n])
                    change = pairs[k][0] * step[n, b] + pairs[k][1] * (inv[n, b] * residual)
                    moved = values[n] + change
                    if k < 1:
                        step[n, b] = change
                    u[n, b] = moved
                    fresh.append(moved)
                if following:
                    width = MODES if k < 1 else CMODES
                    send_x(k + 1, b, [v[0:width] for v in fresh])
            else:
                low = lax.broadcasted_iota(jnp.int32, (CMODES, 8, 128), 0)
                inside_z = jnp.where(low <= (deg[2] >> 1)[None], 1.0, 0.0)
                inside_y = jnp.where((deg[1] >> 1) >= b, 1.0, 0.0)
                mass = (1.0 / ((2.0 * low.astype(F32) + 1.0) * (2.0 * b.astype(F32) + 1.0))) * (
                    inside_z * inside_y[None])
                for n in range(CMODES):
                    inside = jnp.where((deg[0] >> 1) >= n, 8.0 / (2.0 * n + 1.0), 0.0)
                    residual = s[n, b, 0:CMODES] - (acc[n, b, 0:CMODES] + out[n])
                    kept[b, n * 32:(n + 1) * 32] = (residual * (mass * inside[None])).reshape(32, 128)
                fold(b)
            return 0
        if k == 0:
            lax.fori_loop(0, MODES, functools.partial(pass_x, following=True), 0)
        elif k == 1:
            lax.fori_loop(0, CMODES, functools.partial(pass_x, following=True), 0)
            lax.fori_loop(CMODES, MODES, pass_x, 0)
        else:
            lax.fori_loop(0, CMODES, pass_x, 0)

    for d in range(ny):
        @pl.when(gy != d)
        def _(d=d):
            for b in range(CMODES):
                fold_arrival(d, b).wait_recv()
    for d in range(ny):
        left[:, d * 128:(d + 1) * 128] = folded[d].reshape(2 * CMODES**3, 128)
    for d in range(ny):
        @pl.when(gy != d)
        def _(d=d):
            for b in range(CMODES):
                fold_copy(d, b).wait_send()

    for d in range(4):
        @pl.when(exists[d])
        def _(d=d):
            param_copy(d).wait_send()
            make = (x_copy, y_copy)[d // 2]
            for k in range(3):
                def finish(i, _):
                    make(k, d % 2, i).wait_send()
                    return 0
                lax.fori_loop(0, MODES if k < 2 else CMODES, finish, 0)


def smoother(nx, ny, rhs, coef, deg):
    field = pltpu.VMEM((MODES, MODES, MODES, 8, 128), F32)
    wide = pltpu.VMEM((2, 2, MODES, MODES, 8, 128), F32)
    narrow = pltpu.VMEM((2, CMODES, CMODES, 8, 128), F32)
    return pl.pallas_call(
        functools.partial(kernel, nx, ny),
        out_shape=(jax.ShapeDtypeStruct((MODES, MODES, MODES, 8, 128), F32),
                   jax.ShapeDtypeStruct((2 * CMODES**3, ny * 128), F32)),
        in_specs=[pl.BlockSpec(memory_space=pltpu.HBM)] * 3,
        out_specs=[pl.BlockSpec(memory_space=pltpu.VMEM)] * 2,
        scratch_shapes=[
            field,
            pltpu.VMEM((8, 128), F32),
            pltpu.VMEM((3, 8, 128), jnp.int32),
            field, field, field,
            pltpu.VMEM((3, 6, 8, 128), F32),
            pltpu.VMEM((3, MODES, 8, 128), F32),
            pltpu.VMEM((MODES, 8, 128), F32),
            pltpu.VMEM((4, 8, 128), F32),
            pltpu.VMEM((4, 8, 128), F32),
            wide, wide, wide, wide, narrow, narrow, narrow, narrow,
            pltpu.VMEM((CMODES, 128, 128), F32),
            pltpu.VMEM((ny, CMODES, 2, CMODES**2, 128), F32),
            pltpu.VMEM((ny, CMODES, 2, CMODES**2, 128), F32),
            pltpu.SemaphoreType.DMA((3,)),
            pltpu.SemaphoreType.DMA((4,)),
            pltpu.SemaphoreType.DMA((4,)),
            pltpu.SemaphoreType.DMA((3, 2, MODES)),
            pltpu.SemaphoreType.DMA((3, 2, MODES)),
            pltpu.SemaphoreType.DMA((3, 2, MODES)),
            pltpu.SemaphoreType.DMA((3, 2, MODES)),
            pltpu.SemaphoreType.DMA((ny, CMODES)),
            pltpu.SemaphoreType.DMA((ny, CMODES)),
        ],
        compiler_params=pltpu.CompilerParams(
            collective_id=0, has_side_effects=True, vmem_limit_bytes=48 * 1024 * 1024
        ),
    )(*(pltpu.with_memory_space_constraint(v, pltpu.HBM) for v in (rhs, coef, deg)))


def finish_kernel(ny, u, blocks, stored, coarse, order, sem):
    copy = pltpu.make_async_copy(u, stored, sem)
    copy.start()
    depth = 128 // ny
    source_lane = lax.broadcasted_iota(jnp.int32, (128, 512), 0)
    fine_lane = lax.broadcasted_iota(jnp.int32, (128, 512), 1)
    spot = (source_lane % depth) * (4 * ny) + source_lane // depth
    for d in range(ny):
        order[d * 128:(d + 1) * 128] = jnp.where((source_lane < 4 * depth) & (fine_lane == spot + 4 * d), 1.0, 0.0).astype(jnp.bfloat16)
    left = blocks[...]
    total = jnp.zeros((2 * CMODES**3, 512), F32)
    for part in range(3):
        piece = left.astype(jnp.bfloat16)
        total = total + jnp.dot(piece, order[...], preferred_element_type=F32)
        if part < 2:
            left = left - piece.astype(F32)
    for b in range(CMODES):
        for x in range(2):
            for n in range(CMODES):
                for j in range(4):
                    coarse[pl.ds((n * 16 + b * 4) * 8 + j * 2 + x, CMODES, stride=8), :] = total[
                        b * 32 + x * 16 + n * 4:b * 32 + x * 16 + n * 4 + 4, j * 128:(j + 1) * 128]
    copy.wait()


def finish(ny, u, blocks):
    return pl.pallas_call(
        functools.partial(finish_kernel, ny),
        out_shape=(jax.ShapeDtypeStruct(u.shape, F32),
                   jax.ShapeDtypeStruct((CMODES**3 * 8, 128), F32)),
        in_specs=[pl.BlockSpec(memory_space=pl.ANY), pl.BlockSpec(memory_space=pltpu.VMEM)],
        out_specs=[pl.BlockSpec(memory_space=pltpu.HBM), pl.BlockSpec(memory_space=pltpu.VMEM)],
        scratch_shapes=[pltpu.VMEM((ny * 128, 512), jnp.bfloat16), pltpu.SemaphoreType.DMA],
        compiler_params=pltpu.CompilerParams(vmem_limit_bytes=16 * 1024 * 1024),
    )(u, blocks)


def solution(mesh):
    nx, ny = mesh.shape["gx"], mesh.shape["gy"]

    def body(right_side, coefficient, degrees):
        local = right_side.shape[3:]
        flat = (local[0] * local[1], local[2])
        smoothed, blocks = smoother(
            nx, ny,
            right_side.reshape(right_side.shape[:3] + flat),
            coefficient.reshape(flat),
            degrees.reshape((3,) + flat),
        )
        smoothed, coarse = finish(ny, smoothed, blocks)
        coarse = jnp.transpose(coarse.reshape(CMODES**3, 4, 2, 128), (0, 2, 1, 3))
        return smoothed.reshape(right_side.shape), coarse.reshape(CMODES**3, 2, 512)

    in_specs = (
        P(None, None, None, "gx", "gy", None),
        P("gx", "gy", None),
        P(None, "gx", "gy", None),
    )
    out_specs = (P(None, None, None, "gx", "gy", None), P(None, "gx", "gy"))
    return jax.shard_map(body, mesh=mesh, in_specs=in_specs, out_specs=out_specs, check_vma=False)
```
